768 devices in a mesh: occ: 32 (over x_hi, y, core), virt: 24 (over x_lo, z).
Axes of the slice: x: 4 (x_hi: 2, x_lo: 2; x = x_hi * 2 + x_lo), y: 8, z: 12, core: 2. Of those that a mesh axis runs over, the one named last changes fastest.
Arguments:
- amplitudes: bfloat16 [16384, 6144], P('occ'), may hold values from -6 to 6
- amp_map: int32 [256, 48], P('occ'), may hold values 0 or 1
- integrals: bfloat16 [6144, 6144], P('occ', 'virt'), may hold values from -0.078125 to 0.078125
- int_map: int32 [48, 48], P(None, 'virt'), may hold values 0 or 1
- exchange: bfloat16 [16384, 6144], P('occ', 'virt'), may hold values from -0.078125 to 0.078125
- residual_in: float32 [16384, 6144], P('occ', 'virt'), may hold values from -6 to 6
Outputs:
- residual: float32 [16384, 6144], P('occ', 'virt')
- pair_energy: float32 [16384], P('occ')
The draws below stay inside these ranges and needn't reach their ends.
All inputs are finite; a program needn't handle non-finite values. No bound on the sum of `amp_map` or of `int_map` on one device may be relied on, other than what follows from the above.
Results may differ from the reference program's by a relative error of at most 0.0003.
Values may be sent and summed in bfloat16 or wider, within the bound.
No kernel may reach another device: no remote copies, remote signals or barrier semaphores. Data moves between devices by JAX's collectives and lax.ppermute only.
A program may use at most 32 MiB of HBM per device.

```python
import jax
import jax.numpy as jnp
from jax import lax

PTILE = 64
VTILE = 128
PT = 256
KT = 48
PAIRS = 16384
K = 6144


def set_ends(drawn, stream_key, least, top_value):
    longest = drawn.shape.index(max(drawn.shape))
    spots = []
    for shift in (0, 1):
        where = [jax.random.randint(jax.random.fold_in(stream_key, axis), (), 0, length) for axis, length in enumerate(drawn.shape)]
        where[longest] = (where[longest] + shift) % drawn.shape[longest]
        spots.append(tuple(where))
    return drawn.at[spots[0]].set(least).at[spots[1]].set(top_value)


def block_levels(rng, extent, cuts, low, top_value):
    def one(position, shards_of):
        steps = jax.random.uniform(jax.random.fold_in(jax.random.fold_in(rng, 6), position), (shards_of,), jnp.float32, low / len(cuts), top_value / len(cuts))
        return jnp.repeat(jnp.exp(steps), extent[position] // shards_of).reshape((-1,) + (1,) * (len(extent) - position - 1))

    loudness = one(*cuts[0])
    for cut in cuts[1:]:
        loudness = loudness * one(*cut)
    return loudness


def scatter_about(own_key, shape, deviation, limit, shards=(), held_as=jnp.bfloat16):
    array = deviation * jax.random.normal(own_key, shape, jnp.float32)
    if shards:
        array = array * block_levels(own_key, shape, shards, -0.22, 0.18)
    return jnp.clip(array, -limit, limit).astype(held_as)


def setup_inputs(seed: int = 0) -> dict:
    seeds = jax.random.split(jax.random.key(seed), 7)
    return {
        "amplitudes": scatter_about(seeds[0], (PAIRS, K), 1.0, 6.0, ((0, 32),)),
        "amp_map": set_ends((jax.random.randint(seeds[1], (PT, KT), 0, 4) < 3).astype(jnp.int32), jax.random.fold_in(seeds[1], 1), 0, 1),
        "integrals": scatter_about(seeds[2], (K, K), K ** -0.5, 0.078125, ((0, 32), (1, 24))),
        "int_map": set_ends((jax.random.randint(seeds[3], (KT, KT), 0, 4) < 3).astype(jnp.int32), jax.random.fold_in(seeds[3], 1), 0, 1),
        "exchange": scatter_about(seeds[4], (PAIRS, K), K ** -0.5, 0.078125, ((0, 32), (1, 24))),
        "residual_in": scatter_about(seeds[5], (PAIRS, K), 1.0, 6.0, ((0, 32), (1, 24)), jnp.float32),
    }


def expand(table, tall, wide):
    return jnp.repeat(jnp.repeat(table, tall, axis=0), wide, axis=1)


def reference(amplitudes, amp_map, integrals, int_map, exchange, residual_in):
    int_masked = integrals.astype(jnp.float32) * expand(int_map, VTILE, VTILE).astype(jnp.float32)
    tiles = amplitudes.reshape(PT, PTILE, KT, VTILE).astype(jnp.float32)
    tiles = tiles * amp_map.astype(jnp.float32)[:, None, :, None]
    amp_masked = tiles.reshape(PT * PTILE, KT * VTILE)
    product = jnp.dot(amp_masked, int_masked, precision=lax.Precision.HIGHEST, preferred_element_type=jnp.float32)
    residual = residual_in + product
    pair_energy = jnp.sum(residual * exchange.astype(jnp.float32), axis=1)
    return residual, pair_energy
```

```python
import jax
import jax.numpy as jnp
from jax import lax
from jax.sharding import Mesh, PartitionSpec as P

PTILE = 64
VTILE = 128
SCALE = 2.0**19


def on_device(amplitudes, amp_map, integrals, int_map, exchange, residual_in):
    row_tiles, col_tiles = amp_map.shape
    rows, columns = residual_in.shape
    shaped = amplitudes.reshape(row_tiles, PTILE, col_tiles, VTILE)
    amp_masked = (shaped * amp_map.astype(jnp.bfloat16)[:, None, :, None]).reshape(amplitudes.shape)

    mine = (integrals.astype(jnp.float32) * SCALE).astype(jnp.float16)
    pair = lax.all_gather(mine, "xh", axis=0, tiled=False)
    panel = lax.all_gather(pair, ("y", "c"), axis=0, tiled=False)
    panel = panel.swapaxes(0, 1).reshape(-1, columns).astype(jnp.bfloat16)
    full_mask = jnp.repeat(jnp.repeat(int_map, VTILE, axis=0), VTILE, axis=1).astype(jnp.bfloat16)

    product = jnp.dot(amp_masked, panel * full_mask, preferred_element_type=jnp.float32)
    residual = residual_in + product * (1.0 / SCALE)
    terms = jnp.sum(residual * exchange.astype(jnp.float32), axis=1)
    ways = lax.axis_size(("xl", "z"))
    terms = lax.all_to_all(jnp.broadcast_to(terms, (ways, rows)), ("xl", "z"), 0, 0, tiled=True)
    return residual, jnp.sum(terms, axis=0)


def solution(mesh):
    fine = Mesh(mesh.devices.reshape(2, 8, 2, 2, 12), ("xh", "y", "c", "xl", "z"))
    occ, virt = ("xh", "y", "c"), ("xl", "z")
    in_specs = (P(occ, None), P(occ, None), P(occ, virt), P(None, virt), P(occ, virt), P(occ, virt))
    return jax.shard_map(on_device, mesh=fine, in_specs=in_specs, out_specs=(P(occ, virt), P(occ)), check_vma=False)
```

```python
import functools

import jax
import jax.numpy as jnp
from jax import lax
from jax.experimental import pallas as pl
from jax.experimental.pallas import tpu as pltpu
from jax.sharding import Mesh, PartitionSpec as P

PTILE = 64
VTILE = 128
SCALE = 2.0**19


def ladder(shape, amp_map, int_map, amplitudes, panel, exchange, residual_in, residual, terms):
    xh, y, c, part = shape
    rows, columns = residual.shape
    step = 2 * c * part
    chunks = [(h, y0) for h in range(xh) for y0 in range(0, y, 2)]

    total = jnp.zeros((rows, columns), jnp.float32)
    for h, y0 in chunks:
        first = (h * y + y0) * c * part
        right = []
        for at in range(0, step, PTILE):
            block, inner = divmod(at, part)
            source = ((y0 + block // c) * c + block % c) * xh + h
            tiles = []
            for j in range(columns // VTILE):
                keep = int_map[j, (first + at) // VTILE].astype(jnp.bfloat16)
                tiles.append(panel[source, inner : inner + PTILE, j * VTILE : (j + 1) * VTILE] * keep)
            right.append(jnp.concatenate(tiles, axis=1))
        right = jnp.concatenate(right, axis=0)
        left = []
        for r in range(rows // PTILE):
            tiles = []
            for k in range(step // VTILE):
                keep = amp_map[r, first // VTILE + k].astype(jnp.bfloat16)
                tiles.append(amplitudes[r * PTILE : (r + 1) * PTILE, first + k * VTILE : first + (k + 1) * VTILE] * keep)
            left.append(jnp.concatenate(tiles, axis=1))
        left = jnp.concatenate(left, axis=0)
        total += jnp.dot(left, right, preferred_element_type=jnp.float32)
    total = residual_in[...] + total * (1.0 / SCALE)
    residual[...] = total
    product = total * exchange[...].astype(jnp.float32)
    folded = product[:, :VTILE]
    for j in range(1, columns // VTILE):
        folded += product[:, j * VTILE : (j + 1) * VTILE]
    line = jnp.sum(folded.T, axis=0, keepdims=True)
    for i in range(terms.shape[0]):
        terms[i] = line


def on_device(amplitudes, amp_map, integrals, int_map, exchange, residual_in):
    rows, columns = residual_in.shape
    part, depth = integrals.shape[0], amplitudes.shape[1]
    xh, y, c = (lax.axis_size(name) for name in ("xh", "y", "c"))
    ways = lax.axis_size(("xl", "z"))
    mine = (integrals.astype(jnp.float32) * SCALE).astype(jnp.float16)
    pair = lax.all_gather(mine, "xh", axis=0, tiled=False)
    panel = lax.all_gather(pair, ("y", "c"), axis=0, tiled=False)
    panel = panel.reshape(y * c * xh, part, columns).astype(jnp.bfloat16)
    vmem, smem = pl.BlockSpec(memory_space=pltpu.VMEM), pl.BlockSpec(memory_space=pltpu.SMEM)
    residual, terms = pl.pallas_call(
        functools.partial(ladder, (xh, y, c, part)),
        out_shape=(
            jax.ShapeDtypeStruct((rows, columns), jnp.float32),
            jax.ShapeDtypeStruct((ways, 1, rows), jnp.float32),
        ),
        in_specs=[smem, smem, vmem, vmem, vmem, vmem],
        out_specs=(vmem, vmem),
        cost_estimate=pl.CostEstimate(
            flops=2 * rows * depth * columns, bytes_accessed=2 * rows * depth, transcendentals=0
        ),
        compiler_params=pltpu.CompilerParams(vmem_limit_bytes=24 << 20),
        name="ladder",
    )(amp_map, int_map.T, amplitudes, panel, exchange, residual_in)
    terms = lax.all_to_all(terms, ("xl", "z"), 0, 0, tiled=True)
    return residual, jnp.sum(terms, axis=(0, 1))


def solution(mesh):
    fine = Mesh(mesh.devices.reshape(2, 8, 2, 2, 12), ("xh", "y", "c", "xl", "z"))
    occ, virt = ("xh", "y", "c"), ("xl", "z")
    in_specs = (P(occ, None), P(occ, None), P(occ, virt), P(None, virt), P(occ, virt), P(occ, virt))
    return jax.shard_map(on_device, mesh=fine, in_specs=in_specs, out_specs=(P(occ, virt), P(occ)), check_vma=False)
```

```python
import functools

import jax
import jax.numpy as jnp
from jax import lax
from jax.experimental import pallas as pl
from jax.experimental.pallas import tpu as pltpu
from jax.sharding import Mesh, PartitionSpec as P

PTILE = 64
VTILE = 128
SCALE = 2.0**19


def ladder(
    shape, amp_map, int_map, amp_hbm, panel, exchange, residual_in, residual_hbm, terms, amp, residual, in_sems, out_sem
):
    xh, y, c, part = shape
    rows, columns = residual.shape
    step = 2 * c * part
    chunks = [(h, y0) for h in range(xh) for y0 in range(0, y, 2)]

    def fetch(i):
        h, y0 = chunks[i]
        first = (h * y + y0) * c * part
        return pltpu.make_async_copy(amp_hbm.at[:, first : first + step], amp.at[i], in_sems.at[i])

    for i in range(len(chunks)):
        fetch(i).start()
    total = jnp.zeros((rows, columns), jnp.float32)
    for i, (h, y0) in enumerate(chunks):
        first = (h * y + y0) * c * part
        right = []
        for at in range(0, step, PTILE):
            block, inner = divmod(at, part)
            source = ((y0 + block // c) * c + block % c) * xh + h
            tiles = []
            for j in range(columns // VTILE):
                keep = int_map[j, (first + at) // VTILE].astype(jnp.bfloat16)
                tiles.append(panel[source, inner : inner + PTILE, j * VTILE : (j + 1) * VTILE] * keep)
            right.append(jnp.concatenate(tiles, axis=1))
        right = jnp.concatenate(right, axis=0)
        fetch(i).wait()
        left = []
        for r in range(rows // PTILE):
            tiles = []
            for k in range(step // VTILE):
                keep = amp_map[r, first // VTILE + k].astype(jnp.bfloat16)
                tiles.append(amp[i, r * PTILE : (r + 1) * PTILE, k * VTILE : (k + 1) * VTILE] * keep)
            left.append(jnp.concatenate(tiles, axis=1))
        left = jnp.concatenate(left, axis=0)
        total += jnp.dot(left, right, preferred_element_type=jnp.float32)
    total = residual_in[...] + total * (1.0 / SCALE)
    residual[...] = total
    leave = pltpu.make_async_copy(residual, residual_hbm, out_sem)
    leave.start()
    product = total * exchange[...].astype(jnp.float32)
    folded = product[:, :VTILE]
    for j in range(1, columns // VTILE):
        folded += product[:, j * VTILE : (j + 1) * VTILE]
    line = jnp.sum(folded.T, axis=0, keepdims=True)
    for i in range(terms.shape[0]):
        terms[i] = line
    leave.wait()


def on_device(amplitudes, amp_map, integrals, int_map, exchange, residual_in):
    rows, columns = residual_in.shape
    part, depth = integrals.shape[0], amplitudes.shape[1]
    xh, y, c = (lax.axis_size(name) for name in ("xh", "y", "c"))
    ways = lax.axis_size(("xl", "z"))
    pair = lax.all_gather(integrals, "xh", axis=0, tiled=False)
    pair = (pair.astype(jnp.float32) * SCALE).astype(jnp.float16)
    panel = lax.all_gather(pair, ("y", "c"), axis=0, tiled=False)
    panel = panel.reshape(y * c * xh, part, columns).astype(jnp.bfloat16)
    chunks, step = xh * y // 2, 2 * c * part
    vmem, smem = pl.BlockSpec(memory_space=pltpu.VMEM), pl.BlockSpec(memory_space=pltpu.SMEM)
    anywhere = pl.BlockSpec(memory_space=pl.ANY)
    residual, terms = pl.pallas_call(
        functools.partial(ladder, (xh, y, c, part)),
        out_shape=(
            jax.ShapeDtypeStruct((rows, columns), jnp.float32),
            jax.ShapeDtypeStruct((ways, 1, rows), jnp.float32),
        ),
        in_specs=[smem, smem, anywhere, vmem, vmem, vmem],
        out_specs=(anywhere, vmem),
        scratch_shapes=[
            pltpu.VMEM((chunks, rows, step), jnp.bfloat16),
            pltpu.VMEM((rows, columns), jnp.float32),
            pltpu.SemaphoreType.DMA((chunks,)),
            pltpu.SemaphoreType.DMA,
        ],
        cost_estimate=pl.CostEstimate(
            flops=2 * rows * depth * columns, bytes_accessed=2 * rows * depth, transcendentals=0
        ),
        compiler_params=pltpu.CompilerParams(vmem_limit_bytes=50 << 20),
        name="ladder",
    )(amp_map, int_map.T, amplitudes, panel, exchange, residual_in)
    terms = lax.all_to_all(terms, ("xl", "z"), 0, 0, tiled=True)
    return residual, jnp.sum(terms, axis=(0, 1))


def solution(mesh):
    fine = Mesh(mesh.devices.reshape(2, 8, 2, 2, 12), ("xh", "y", "c", "xl", "z"))
    occ, virt = ("xh", "y", "c"), ("xl", "z")
    in_specs = (P(occ, None), P(occ, None), P(occ, virt), P(None, virt), P(occ, virt), P(occ, virt))
    return jax.shard_map(on_device, mesh=fine, in_specs=in_specs, out_specs=(P(occ, virt), P(occ)), check_vma=False)
```

```python
import functools

import jax
import jax.numpy as jnp
from jax import lax
from jax.experimental import pallas as pl
from jax.experimental.pallas import tpu as pltpu
from jax.sharding import Mesh, PartitionSpec as P

PTILE = 64
VTILE = 128
SCALE = 2.0**19


def ladder(shape, amp_map, int_map, amplitudes, panel, exchange, residual_in, residual, terms):
    xh, y, c, part = shape
    rows, columns = residual.shape
    step = 2 * c * part
    chunks = [(h, y0) for h in range(xh) for y0 in range(0, y, 2)]

    total = jnp.zeros((rows, columns), jnp.float32)
    for h, y0 in chunks:
        first = (h * y + y0) * c * part
        right = []
        for at in range(0, step, PTILE):
            block, inner = divmod(at, part)
            source = ((y0 + block // c) * c + block % c) * xh + h
            tiles = []
            for j in range(columns // VTILE):
                keep = int_map[j, (first + at) // VTILE].astype(jnp.bfloat16)
                tiles.append(panel[source, inner : inner + PTILE, j * VTILE : (j + 1) * VTILE] * keep)
            right.append(jnp.concatenate(tiles, axis=1))
        right = jnp.concatenate(right, axis=0)
        left = []
        for r in range(rows // PTILE):
            tiles = []
            for k in range(step // VTILE):
                keep = amp_map[r, first // VTILE + k].astype(jnp.bfloat16)
                tiles.append(amplitudes[r * PTILE : (r + 1) * PTILE, first + k * VTILE : first + (k + 1) * VTILE] * keep)
            left.append(jnp.concatenate(tiles, axis=1))
        left = jnp.concatenate(left, axis=0)
        total += jnp.dot(left, right, preferred_element_type=jnp.float32)
    total = residual_in[...] + total * (1.0 / SCALE)
    residual[...] = total
    product = total * exchange[...].astype(jnp.float32)
    folded = product[:, :VTILE]
    for j in range(1, columns // VTILE):
        folded += product[:, j * VTILE : (j + 1) * VTILE]
    line = jnp.sum(folded.T, axis=0, keepdims=True)
    for i in range(terms.shape[0]):
        terms[i] = line


def on_device(amplitudes, amp_map, integrals, int_map, exchange, residual_in):
    rows, columns = residual_in.shape
    part, depth = integrals.shape[0], amplitudes.shape[1]
    xh, y, c = (lax.axis_size(name) for name in ("xh", "y", "c"))
    ways = lax.axis_size(("xl", "z"))
    pair = lax.all_gather(integrals, "xh", axis=0, tiled=False)
    pair = (pair.astype(jnp.float32) * SCALE).astype(jnp.float16)
    panel = lax.all_gather(pair, ("y", "c"), axis=0, tiled=False)
    panel = panel.reshape(y * c * xh, part, columns).astype(jnp.bfloat16)
    vmem, smem = pl.BlockSpec(memory_space=pltpu.VMEM), pl.BlockSpec(memory_space=pltpu.SMEM)
    residual, terms = pl.pallas_call(
        functools.partial(ladder, (xh, y, c, part)),
        out_shape=(
            jax.ShapeDtypeStruct((rows, columns), jnp.float32),
            jax.ShapeDtypeStruct((ways, 1, rows), jnp.float32),
        ),
        in_specs=[smem, smem, vmem, vmem, vmem, vmem],
        out_specs=(vmem, vmem),
        cost_estimate=pl.CostEstimate(
            flops=2 * rows * depth * columns, bytes_accessed=2 * rows * depth, transcendentals=0
        ),
        compiler_params=pltpu.CompilerParams(vmem_limit_bytes=24 << 20),
        name="ladder",
    )(amp_map, int_map.T, amplitudes, panel, exchange, residual_in)
    terms = lax.all_to_all(terms, ("xl", "z"), 0, 0, tiled=True)
    return residual, jnp.sum(terms, axis=(0, 1))


def solution(mesh):
    fine = Mesh(mesh.devices.reshape(2, 8, 2, 2, 12), ("xh", "y", "c", "xl", "z"))
    occ, virt = ("xh", "y", "c"), ("xl", "z")
    in_specs = (P(occ, None), P(occ, None), P(occ, virt), P(None, virt), P(occ, virt), P(occ, virt))
    return jax.shard_map(on_device, mesh=fine, in_specs=in_specs, out_specs=(P(occ, virt), P(occ)), check_vma=False)
```

```python
import functools

import jax
import jax.numpy as jnp
from jax import lax
from jax.experimental import pallas as pl
from jax.experimental.pallas import tpu as pltpu
from jax.sharding import Mesh, PartitionSpec as P

PTILE = 64
VTILE = 128
EARLY = 6
SCALE = 2.0**19


def multiply(shape, start, amp_map, int_map, amplitudes, panel):
    xh, y, c, part = shape
    rows, columns = amplitudes.shape[0], panel.shape[2]
    step = 2 * c * part
    total = jnp.zeros((rows, columns), jnp.float32)
    for h, y0 in [(h, y0) for h in range(xh) for y0 in range(0, panel.shape[0] // (c * xh), 2)]:
        first = (h * y + start + y0) * c * part
        right = []
        for at in range(0, step, PTILE):
            block, inner = divmod(at, part)
            source = ((y0 + block // c) * c + block % c) * xh + h
            tiles = []
            for j in range(columns // VTILE):
                keep = int_map[j, (first + at) // VTILE].astype(jnp.bfloat16)
                tiles.append(panel[source, inner : inner + PTILE, j * VTILE : (j + 1) * VTILE] * keep)
            right.append(jnp.concatenate(tiles, axis=1))
        right = jnp.concatenate(right, axis=0)
        left = []
        for r in range(rows // PTILE):
            tiles = []
            for k in range(step // VTILE):
                keep = amp_map[r, first // VTILE + k].astype(jnp.bfloat16)
                at = first + k * VTILE
                tiles.append(amplitudes[r * PTILE : (r + 1) * PTILE, at : at + VTILE] * keep)
            left.append(jnp.concatenate(tiles, axis=1))
        left = jnp.concatenate(left, axis=0)
        total += jnp.dot(left, right, preferred_element_type=jnp.float32)
    return total * (1.0 / SCALE)


def opening(shape, start, amp_map, int_map, amplitudes, panel, partial):
    partial[...] = multiply(shape, start, amp_map, int_map, amplitudes, panel)


def closing(
    shape, start, amp_map, int_map, amplitudes, panel, partial, residual_in, exchange, residual_hbm, terms, residual, sem
):
    total = residual_in[...] + (partial[...] + multiply(shape, start, amp_map, int_map, amplitudes, panel))
    residual[...] = total
    leave = pltpu.make_async_copy(residual, residual_hbm, sem)
    leave.start()
    product = total * exchange[...].astype(jnp.float32)
    folded = product[:, :VTILE]
    for j in range(1, product.shape[1] // VTILE):
        folded += product[:, j * VTILE : (j + 1) * VTILE]
    line = jnp.sum(folded.T, axis=0, keepdims=True)
    for i in range(terms.shape[0]):
        terms[i] = line
    leave.wait()


def on_device(amplitudes, amp_map, integrals, int_map, exchange, residual_in):
    rows, columns = residual_in.shape
    part, depth = integrals.shape[0], amplitudes.shape[1]
    xh, y, c = (lax.axis_size(name) for name in ("xh", "y", "c"))
    ways = lax.axis_size(("xl", "z"))
    pair = lax.all_gather(integrals, "xh", axis=0, tiled=False)
    pair = (pair.astype(jnp.float32) * SCALE).astype(jnp.float16)
    panel = lax.all_gather(pair, ("y", "c"), axis=0, tiled=False)
    panel = panel.reshape(y * c * xh, part, columns)
    vmem, smem = pl.BlockSpec(memory_space=pltpu.VMEM), pl.BlockSpec(memory_space=pltpu.SMEM)

    def call(body, start, stop, outs, specs, others, scratch=()):
        share = depth * (stop - start) // y
        return pl.pallas_call(
            functools.partial(body, (xh, y, c, part), start),
            out_shape=outs,
            in_specs=[smem, smem, vmem, vmem] + [vmem] * len(others),
            out_specs=specs,
            scratch_shapes=scratch,
            cost_estimate=pl.CostEstimate(
                flops=2 * rows * share * columns, bytes_accessed=2 * rows * share, transcendentals=0
            ),
            compiler_params=pltpu.CompilerParams(vmem_limit_bytes=24 << 20),
            name=body.__name__,
        )(amp_map, int_map.T, amplitudes, panel[start * c * xh : stop * c * xh].astype(jnp.bfloat16), *others)

    block = jax.ShapeDtypeStruct((rows, columns), jnp.float32)
    lines = jax.ShapeDtypeStruct((ways, 1, rows), jnp.float32)
    partial = call(opening, 0, EARLY, block, vmem, ())
    partial, panel = lax.optimization_barrier((partial, panel))
    residual, terms = call(
        closing,
        EARLY,
        y,
        (block, lines),
        (pl.BlockSpec(memory_space=pl.ANY), vmem),
        (partial, residual_in, exchange),
        [pltpu.VMEM((rows, columns), jnp.float32), pltpu.SemaphoreType.DMA],
    )
    terms = lax.all_to_all(terms, ("xl", "z"), 0, 0, tiled=True)
    return residual, jnp.sum(terms, axis=(0, 1))


def solution(mesh):
    fine = Mesh(mesh.devices.reshape(2, 8, 2, 2, 12), ("xh", "y", "c", "xl", "z"))
    occ, virt = ("xh", "y", "c"), ("xl", "z")
    in_specs = (P(occ, None), P(occ, None), P(occ, virt), P(None, virt), P(occ, virt), P(occ, virt))
    return jax.shard_map(on_device, mesh=fine, in_specs=in_specs, out_specs=(P(occ, virt), P(occ)), check_vma=False)
```

```python
import functools

import jax
import jax.numpy as jnp
from jax import lax
from jax.experimental import pallas as pl
from jax.experimental.pallas import tpu as pltpu
from jax.sharding import Mesh, PartitionSpec as P

PTILE = 64
VTILE = 128
EARLY = 4
SCALE = 2.0**19


def touch(amplitudes, near, residual_in, exchange, token):
    token[...] = amplitudes[: token.shape[0], : token.shape[1]]


def ladder(
    shape, amp_map, int_map, amplitudes, near, far, token, residual_in, exchange, residual_hbm, terms, residual, sems
):
    xh, y, c, part = shape
    rows, columns = residual.shape
    step = 2 * c * part
    total = jnp.zeros((rows, columns), jnp.float32)
    for panel, start in ((near, 0), (far, EARLY)):
        for h, y0 in [(h, y0) for h in range(xh) for y0 in range(0, panel.shape[0] // (c * xh), 2)]:
            first = (h * y + start + y0) * c * part
            right = []
            for at in range(0, step, PTILE):
                block, inner = divmod(at, part)
                source = ((y0 + block // c) * c + block % c) * xh + h
                tiles = []
                for j in range(columns // VTILE):
                    keep = int_map[j, (first + at) // VTILE].astype(jnp.bfloat16)
                    tiles.append(panel[source, inner : inner + PTILE, j * VTILE : (j + 1) * VTILE] * keep)
                right.append(jnp.concatenate(tiles, axis=1))
            right = jnp.concatenate(right, axis=0)
            left = []
            for r in range(rows // PTILE):
                tiles = []
                for k in range(step // VTILE):
                    keep = amp_map[r, first // VTILE + k].astype(jnp.bfloat16)
                    at = first + k * VTILE
                    tiles.append(amplitudes[r * PTILE : (r + 1) * PTILE, at : at + VTILE] * keep)
                left.append(jnp.concatenate(tiles, axis=1))
            left = jnp.concatenate(left, axis=0)
            total += jnp.dot(left, right, preferred_element_type=jnp.float32)
    total = residual_in[...] + total * (1.0 / SCALE)
    some = rows // sems.shape[0]
    leaving = []
    for i in range(sems.shape[0]):
        block = pl.ds(i * some, some)
        residual[block] = total[i * some : (i + 1) * some]
        leaving.append(pltpu.make_async_copy(residual.at[block], residual_hbm.at[block], sems.at[i]))
        leaving[-1].start()
    product = total * exchange[...].astype(jnp.float32)
    folded = product[:, :VTILE]
    for j in range(1, columns // VTILE):
        folded += product[:, j * VTILE : (j + 1) * VTILE]
    line = jnp.sum(folded.T, axis=0, keepdims=True)
    for i in range(terms.shape[0]):
        terms[i] = line
    for copy in leaving:
        copy.wait()


def on_device(amplitudes, amp_map, integrals, int_map, exchange, residual_in):
    rows, columns = residual_in.shape
    part, depth = integrals.shape[0], amplitudes.shape[1]
    xh, y, c = (lax.axis_size(name) for name in ("xh", "y", "c"))
    ways = lax.axis_size(("xl", "z"))
    pair = lax.all_gather(integrals, "xh", axis=0, tiled=False)
    pair = (pair.astype(jnp.float32) * SCALE).astype(jnp.float16)
    panel = lax.all_gather(pair, ("y", "c"), axis=0, tiled=False)
    panel = panel.reshape(y * c * xh, part, columns)
    vmem, smem = pl.BlockSpec(memory_space=pltpu.VMEM), pl.BlockSpec(memory_space=pltpu.SMEM)

    cut = EARLY * c * xh
    near = panel[:cut].astype(jnp.bfloat16)
    token = pl.pallas_call(
        touch,
        out_shape=jax.ShapeDtypeStruct((16, VTILE), amplitudes.dtype),
        in_specs=[vmem] * 4,
        out_specs=vmem,
        compiler_params=pltpu.CompilerParams(vmem_limit_bytes=4 << 20),
        name="touch",
    )(amplitudes, near, residual_in, exchange)
    near, token, panel = lax.optimization_barrier((near, token, panel))
    far = panel[cut:].astype(jnp.bfloat16)
    residual, terms = pl.pallas_call(
        functools.partial(ladder, (xh, y, c, part)),
        out_shape=(
            jax.ShapeDtypeStruct((rows, columns), jnp.float32),
            jax.ShapeDtypeStruct((ways, 1, rows), jnp.float32),
        ),
        in_specs=[smem, smem] + [vmem] * 6,
        out_specs=(pl.BlockSpec(memory_space=pl.ANY), vmem),
        scratch_shapes=[pltpu.VMEM((rows, columns), jnp.float32), pltpu.SemaphoreType.DMA((4,))],
        cost_estimate=pl.CostEstimate(
            flops=2 * rows * depth * columns, bytes_accessed=2 * rows * depth, transcendentals=0
        ),
        compiler_params=pltpu.CompilerParams(vmem_limit_bytes=24 << 20),
        name="ladder",
    )(amp_map, int_map.T, amplitudes, near, far, token, residual_in, exchange)
    terms = lax.all_to_all(terms, ("xl", "z"), 0, 0, tiled=True)
    return residual, jnp.sum(terms, axis=(0, 1))


def solution(mesh):
    fine = Mesh(mesh.devices.reshape(2, 8, 2, 2, 12), ("xh", "y", "c", "xl", "z"))
    occ, virt = ("xh", "y", "c"), ("xl", "z")
    in_specs = (P(occ, None), P(occ, None), P(occ, virt), P(None, virt), P(occ, virt), P(occ, virt))
    return jax.shard_map(on_device, mesh=fine, in_specs=in_specs, out_specs=(P(occ, virt), P(occ)), check_vma=False)
```

```python
import functools

import jax
import jax.numpy as jnp
from jax import lax
from jax.experimental import pallas as pl
from jax.experimental.pallas import tpu as pltpu
from jax.sharding import Mesh, PartitionSpec as P

PTILE = 64
VTILE = 128
EARLY = 4
SCALE = 2.0**19


def touch(amplitudes, near, residual_in, exchange, amp_map, int_map, token):
    token[...] = amplitudes[: token.shape[0], : token.shape[1]]


def ladder(
    shape, amp_map, int_map, amplitudes, near, far, token, residual_in, exchange, residual_hbm, terms, residual, sems
):
    xh, y, c, part = shape
    rows, columns = residual.shape
    step = 2 * c * part
    total = jnp.zeros((rows, columns), jnp.float32)
    for panel, start in ((near, 0), (far, EARLY)):
        for h, y0 in [(h, y0) for h in range(xh) for y0 in range(0, panel.shape[0] // (c * xh), 2)]:
            first = (h * y + start + y0) * c * part
            right = []
            for at in range(0, step, PTILE):
                block, inner = divmod(at, part)
                source = ((y0 + block // c) * c + block % c) * xh + h
                tiles = []
                for j in range(columns // VTILE):
                    keep = int_map[j, (first + at) // VTILE].astype(jnp.bfloat16)
                    tiles.append(panel[source, inner : inner + PTILE, j * VTILE : (j + 1) * VTILE] * keep)
                right.append(jnp.concatenate(tiles, axis=1))
            right = jnp.concatenate(right, axis=0)
            left = []
            for r in range(rows // PTILE):
                tiles = []
                for k in range(step // VTILE):
                    keep = amp_map[r, first // VTILE + k].astype(jnp.bfloat16)
                    at = first + k * VTILE
                    tiles.append(amplitudes[r * PTILE : (r + 1) * PTILE, at : at + VTILE] * keep)
                left.append(jnp.concatenate(tiles, axis=1))
            left = jnp.concatenate(left, axis=0)
            total += jnp.dot(left, right, preferred_element_type=jnp.float32)
    total = residual_in[...] + total * (1.0 / SCALE)
    some = rows // sems.shape[0]
    leaving = []
    for i in range(sems.shape[0]):
        block = pl.ds(i * some, some)
        residual[block] = total[i * some : (i + 1) * some]
        leaving.append(pltpu.make_async_copy(residual.at[block], residual_hbm.at[block], sems.at[i]))
        leaving[-1].start()
    product = total * exchange[...].astype(jnp.float32)
    folded = product[:, :VTILE]
    for j in range(1, columns // VTILE):
        folded += product[:, j * VTILE : (j + 1) * VTILE]
    line = jnp.sum(folded.T, axis=0, keepdims=True)
    for i in range(terms.shape[0]):
        terms[i] = line
    for copy in leaving:
        copy.wait()


def on_device(amplitudes, amp_map, integrals, int_map, exchange, residual_in):
    rows, columns = residual_in.shape
    part, depth = integrals.shape[0], amplitudes.shape[1]
    xh, y, c = (lax.axis_size(name) for name in ("xh", "y", "c"))
    ways = lax.axis_size(("xl", "z"))
    pair = lax.all_gather(integrals, "xh", axis=0, tiled=False)
    pair = (pair.astype(jnp.float32) * SCALE).astype(jnp.float16)
    panel = lax.all_gather(pair, ("y", "c"), axis=0, tiled=False)
    panel = panel.reshape(y * c * xh, part, columns)
    vmem, smem = pl.BlockSpec(memory_space=pltpu.VMEM), pl.BlockSpec(memory_space=pltpu.SMEM)

    cut = EARLY * c * xh
    near = panel[:cut].astype(jnp.bfloat16)
    token = pl.pallas_call(
        touch,
        out_shape=jax.ShapeDtypeStruct((16, VTILE), amplitudes.dtype),
        in_specs=[vmem] * 6,
        out_specs=vmem,
        compiler_params=pltpu.CompilerParams(vmem_limit_bytes=4 << 20),
        name="touch",
    )(amplitudes, near, residual_in, exchange, amp_map, int_map.T)
    near, token, panel = lax.optimization_barrier((near, token, panel))
    far = panel[cut:].astype(jnp.bfloat16)
    residual, terms = pl.pallas_call(
        functools.partial(ladder, (xh, y, c, part)),
        out_shape=(
            jax.ShapeDtypeStruct((rows, columns), jnp.float32),
            jax.ShapeDtypeStruct((ways, 1, rows), jnp.float32),
        ),
        in_specs=[smem, smem] + [vmem] * 6,
        out_specs=(pl.BlockSpec(memory_space=pl.ANY), vmem),
        scratch_shapes=[pltpu.VMEM((rows, columns), jnp.float32), pltpu.SemaphoreType.DMA((4,))],
        cost_estimate=pl.CostEstimate(
            flops=2 * rows * depth * columns, bytes_accessed=2 * rows * depth, transcendentals=0
        ),
        compiler_params=pltpu.CompilerParams(vmem_limit_bytes=24 << 20),
        name="ladder",
    )(amp_map, int_map.T, amplitudes, near, far, token, residual_in, exchange)
    terms = lax.all_to_all(terms, ("xl", "z"), 0, 0, tiled=True)
    return residual, jnp.sum(terms, axis=(0, 1))


def solution(mesh):
    fine = Mesh(mesh.devices.reshape(2, 8, 2, 2, 12), ("xh", "y", "c", "xl", "z"))
    occ, virt = ("xh", "y", "c"), ("xl", "z")
    in_specs = (P(occ, None), P(occ, None), P(occ, virt), P(None, virt), P(occ, virt), P(occ, virt))
    return jax.shard_map(on_device, mesh=fine, in_specs=in_specs, out_specs=(P(occ, virt), P(occ)), check_vma=False)
```

```python
import functools

import jax
import jax.numpy as jnp
from jax import lax
from jax.experimental import pallas as pl
from jax.experimental.pallas import tpu as pltpu
from jax.sharding import Mesh, PartitionSpec as P

PTILE = 64
VTILE = 128
EARLY = 4
SCALE = 2.0**19


def touch(amplitudes, near, residual_in, exchange, token):
    token[...] = amplitudes[: token.shape[0], : token.shape[1]]


def ladder(
    shape, amp_map, int_map, amplitudes, near, far, token, residual_in, exchange, residual_hbm, terms, residual, sems
):
    xh, y, c, part = shape
    rows, columns = residual.shape
    step = 2 * c * part
    total = jnp.zeros((rows, columns), jnp.float32)
    for panel, start in ((near, 0), (far, EARLY)):
        for h, y0 in [(h, y0) for h in range(xh) for y0 in range(0, panel.shape[0] // (c * xh), 2)]:
            first = (h * y + start + y0) * c * part
            right = []
            for at in range(0, step, PTILE):
                block, inner = divmod(at, part)
                source = ((y0 + block // c) * c + block % c) * xh + h
                tiles = []
                for j in range(columns // VTILE):
                    keep = int_map[j, (first + at) // VTILE].astype(jnp.bfloat16)
                    tiles.append(panel[source, inner : inner + PTILE, j * VTILE : (j + 1) * VTILE] * keep)
                right.append(jnp.concatenate(tiles, axis=1))
            right = jnp.concatenate(right, axis=0)
            left = []
            for r in range(rows // PTILE):
                tiles = []
                for k in range(step // VTILE):
                    keep = amp_map[r, first // VTILE + k].astype(jnp.bfloat16)
                    at = first + k * VTILE
                    tiles.append(amplitudes[r * PTILE : (r + 1) * PTILE, at : at + VTILE] * keep)
                left.append(jnp.concatenate(tiles, axis=1))
            left = jnp.concatenate(left, axis=0)
            total += jnp.dot(left, right, preferred_element_type=jnp.float32)
    total = residual_in[...] + total * (1.0 / SCALE)
    some = rows // sems.shape[0]
    leaving = []
    for i in range(sems.shape[0]):
        block = pl.ds(i * some, some)
        residual[block] = total[i * some : (i + 1) * some]
        leaving.append(pltpu.make_async_copy(residual.at[block], residual_hbm.at[block], sems.at[i]))
        leaving[-1].start()
    product = total * exchange[...].astype(jnp.float32)
    folded = product[:, :VTILE]
    for j in range(1, columns // VTILE):
        folded += product[:, j * VTILE : (j + 1) * VTILE]
    line = jnp.sum(folded.T, axis=0, keepdims=True)
    for i in range(terms.shape[0]):
        terms[i] = line
    for copy in leaving:
        copy.wait()


def on_device(amplitudes, amp_map, integrals, int_map, exchange, residual_in):
    rows, columns = residual_in.shape
    part, depth = integrals.shape[0], amplitudes.shape[1]
    xh, y, c = (lax.axis_size(name) for name in ("xh", "y", "c"))
    ways = lax.axis_size(("xl", "z"))
    pair = lax.all_gather(integrals, "xh", axis=0, tiled=False)
    pair = (pair.astype(jnp.float32) * SCALE).astype(jnp.float16)
    panel = lax.all_gather(pair, ("y", "c"), axis=0, tiled=False)
    panel = panel.reshape(y * c * xh, part, columns)
    vmem, smem = pl.BlockSpec(memory_space=pltpu.VMEM), pl.BlockSpec(memory_space=pltpu.SMEM)

    cut = EARLY * c * xh
    near = panel[:cut].astype(jnp.bfloat16)
    token = pl.pallas_call(
        touch,
        out_shape=jax.ShapeDtypeStruct((16, VTILE), amplitudes.dtype),
        in_specs=[vmem] * 4,
        out_specs=vmem,
        compiler_params=pltpu.CompilerParams(vmem_limit_bytes=4 << 20),
        name="touch",
    )(amplitudes, near, residual_in, exchange)
    near, token, panel = lax.optimization_barrier((near, token, panel))
    far = panel[cut:].astype(jnp.bfloat16)
    residual, terms = pl.pallas_call(
        functools.partial(ladder, (xh, y, c, part)),
        out_shape=(
            jax.ShapeDtypeStruct((rows, columns), jnp.float32),
            jax.ShapeDtypeStruct((ways, 1, rows), jnp.float32),
        ),
        in_specs=[smem, smem] + [vmem] * 6,
        out_specs=(pl.BlockSpec(memory_space=pl.ANY), vmem),
        scratch_shapes=[pltpu.VMEM((rows, columns), jnp.float32), pltpu.SemaphoreType.DMA((8,))],
        cost_estimate=pl.CostEstimate(
            flops=2 * rows * depth * columns, bytes_accessed=2 * rows * depth, transcendentals=0
        ),
        compiler_params=pltpu.CompilerParams(vmem_limit_bytes=24 << 20),
        name="ladder",
    )(amp_map, int_map.T, amplitudes, near, far, token, residual_in, exchange)
    terms = lax.all_to_all(terms, ("xl", "z"), 0, 0, tiled=True)
    return residual, jnp.sum(terms, axis=(0, 1))


def solution(mesh):
    fine = Mesh(mesh.devices.reshape(2, 8, 2, 2, 12), ("xh", "y", "c", "xl", "z"))
    occ, virt = ("xh", "y", "c"), ("xl", "z")
    in_specs = (P(occ, None), P(occ, None), P(occ, virt), P(None, virt), P(occ, virt), P(occ, virt))
    return jax.shard_map(on_device, mesh=fine, in_specs=in_specs, out_specs=(P(occ, virt), P(occ)), check_vma=False)
```
